32 devices in a mesh: dp: 8 (over z, x), tensor: 4 (over y, core).
Axes of the slice: x: 2, y: 2, z: 4, core: 2. Of those that a mesh axis runs over, the one named last changes fastest.
Arguments:
- layer_input: bfloat16 [4096, 768], P(('dp', 'tensor')), may hold values from -24 to 24
- out_grad: bfloat16 [4096, 768], P(('dp', 'tensor')), may hold values from -6 to 6
- qkv_weight: float32 [2, 3, 768, 768], P(None, None, 'dp', 'tensor'), may hold values from -0.5 to 0.5
- qv_bias: float32 [2, 2, 768], P(None, None, ('tensor', 'dp')), may hold values from -0.8 to 0.8
- proj_weight: float32 [2, 768, 768], P(None, 'tensor', 'dp'), may hold values from -1 to 1
- up_weight: float32 [2, 768, 3072], P(None, 'dp', 'tensor'), may hold values from -0.21875 to 0.21875
- up_bias: float32 [2, 3072], P(None, ('tensor', 'dp')), may hold values from -0.8 to 0.8
- down_weight: float32 [2, 3072, 768], P(None, 'tensor', 'dp'), may hold values from -0.109375 to 0.109375
- norm_vectors: float32 [2, 6, 768], P(None, None, 'dp'), may hold values from -0.8 to 1.6, as said below
- qkv_moments: float32 [2, 2, 3, 768, 768], P(None, None, None, 'dp', 'tensor'), may hold values from -7.68 to 7.68, as said below
- qvbias_moments: float32 [2, 2, 2, 768], P(None, None, None, ('tensor', 'dp')), may hold values from -7.68 to 7.68, as said below
- proj_moments: float32 [2, 2, 768, 768], P(None, None, 'tensor', 'dp'), may hold values from -1.28 to 1.28, as said below
- up_moments: float32 [2, 2, 768, 3072], P(None, None, 'dp', 'tensor'), may hold values from -7.68 to 7.68, as said below
- upbias_moments: float32 [2, 2, 3072], P(None, None, ('tensor', 'dp')), may hold values from -7.68 to 7.68, as said below
- down_moments: float32 [2, 2, 3072, 768], P(None, None, 'tensor', 'dp'), may hold values from -7.68 to 7.68, as said below
- vector_moments: float32 [2, 2, 6, 768], P(None, None, None, 'dp'), may hold values from -20.48 to 20.48, as said below
Outputs:
- block_output: bfloat16 [4096, 768], P(('dp', 'tensor'))
- input_grad: float32 [4096, 768], P(('dp', 'tensor'))
- qkv_grad: float32 [2, 3, 768, 768], P(None, None, 'dp', 'tensor')
- qvbias_grad: float32 [2, 2, 768], P(None, None, ('tensor', 'dp'))
- proj_grad: float32 [2, 768, 768], P(None, 'tensor', 'dp')
- up_grad: float32 [2, 768, 3072], P(None, 'dp', 'tensor')
- upbias_grad: float32 [2, 3072], P(None, ('tensor', 'dp'))
- down_grad: float32 [2, 3072, 768], P(None, 'tensor', 'dp')
- vector_grad: float32 [2, 6, 768], P(None, None, 'dp')
- qkv_updated: float32 [2, 3, 768, 768], P(None, None, 'dp', 'tensor')
- qvbias_updated: float32 [2, 2, 768], P(None, None, ('tensor', 'dp'))
- proj_updated: float32 [2, 768, 768], P(None, 'tensor', 'dp')
- up_updated: float32 [2, 768, 3072], P(None, 'dp', 'tensor')
- upbias_updated: float32 [2, 3072], P(None, ('tensor', 'dp'))
- down_updated: float32 [2, 3072, 768], P(None, 'tensor', 'dp')
- vector_updated: float32 [2, 6, 768], P(None, None, 'dp')
- qkv_states: float32 [2, 2, 3, 768, 768], P(None, None, None, 'dp', 'tensor')
- qvbias_states: float32 [2, 2, 2, 768], P(None, None, None, ('tensor', 'dp'))
- proj_states: float32 [2, 2, 768, 768], P(None, None, 'tensor', 'dp')
- up_states: float32 [2, 2, 768, 3072], P(None, None, 'dp', 'tensor')
- upbias_states: float32 [2, 2, 3072], P(None, None, ('tensor', 'dp'))
- down_states: float32 [2, 2, 3072, 768], P(None, None, 'tensor', 'dp')
- vector_states: float32 [2, 2, 6, 768], P(None, None, None, 'dp')
The draws below stay inside these ranges and needn't reach their ends.
Inputs may be any that keep to these rules, and one draw needn't show every extreme that they name: `norm_vectors`: gain rows lie in 0.4 to 1.6. `qkv_moments`: index 0 of the first dimension holds first moments, index 1 second moments, which are positive. `qvbias_moments`: index 0 of the first dimension holds first moments, index 1 second moments, which are positive. `proj_moments`: index 0 of the first dimension holds first moments, index 1 second moments, which are positive. `up_moments`: index 0 of the first dimension holds first moments, index 1 second moments, which are positive. `upbias_moments`: index 0 of the first dimension holds first moments, index 1 second moments, which are positive. `down_moments`: index 0 of the first dimension holds first moments, index 1 second moments, which are positive. `vector_moments`: index 0 of the first dimension holds first moments, index 1 second moments, which are positive.
All inputs are finite; a program needn't handle non-finite values.
Results may differ from the reference program's by a relative error of at most 0.035.
The reference program's roundings to bfloat16 on the way count: a program that leaves them out, or rounds other values in their place, can miss the bound.
Values may be sent and summed in bfloat16 or wider, within the bound.
No kernel may reach another device: no remote copies, remote signals or barrier semaphores. Data moves between devices by JAX's collectives and lax.ppermute only.
A program may use at most 128 MiB of HBM per device.

```python
import jax
import jax.numpy as jnp
from jax import lax

D = 768
HEAD_DIM = 64
FF = 3072
LAYERS = 2
SEQ_DP = 2
SEQ_LEN = 256
ADAM_STEP = 3
TOKENS = 4096
N_DP = 8


def draw_layer_input(key, part):
    normals = jnp.clip(jax.random.normal(key, (TOKENS, D), jnp.float32), -6.0, 6.0)
    return normals.astype(jnp.bfloat16)


def draw_qkv_weight(key, part):
    key = jax.random.fold_in(key, 31)
    normals = jnp.clip(jax.random.normal(key, (LAYERS, 3, D, D), jnp.float32), -4.0, 4.0) * D ** (-0.5)
    return jnp.clip(normals, -0.5, 0.5)


def draw_norm_vectors(key, part):
    key = jax.random.fold_in(key, 41)
    normals = jnp.clip(jax.random.normal(key, (LAYERS, 6, D), jnp.float32), -4.0, 4.0)
    rows_at = jnp.arange(6)
    gain_rows = ((rows_at == 1) | (rows_at == 4))[None, :, None]
    return jnp.where(gain_rows, 1.0 + 0.15 * normals, 0.2 * normals).astype(jnp.float32)


def moment_pair(key, tag, shape, spread):
    key = jax.random.fold_in(key, tag)
    scaling = spread * TOKENS ** 0.5
    first_mom = 0.1 * scaling * jnp.clip(jax.random.normal(jax.random.fold_in(key, 21), shape, jnp.float32), -4.0, 4.0)
    factors = jnp.exp(jax.random.uniform(jax.random.fold_in(key, 22), shape, jnp.float32, -1.3862944, 1.3862944))
    second_mom = 0.001 * scaling * scaling * factors
    return jnp.stack([first_mom, second_mom]).astype(jnp.float32)


def draw_qkv_moments(key, part):
    return moment_pair(key, 101, (LAYERS, 3, D, D), 0.3)


def draw_qvbias_moments(key, part):
    return moment_pair(key, 102, (LAYERS, 2, D), 0.3)


def draw_proj_moments(key, part):
    return moment_pair(key, 103, (LAYERS, D, D), 0.05)


def draw_up_moments(key, part):
    return moment_pair(key, 104, (LAYERS, D, FF), 0.3)


def draw_upbias_moments(key, part):
    return moment_pair(key, 105, (LAYERS, FF), 0.3)


def draw_down_moments(key, part):
    return moment_pair(key, 106, (LAYERS, FF, D), 0.3)


def draw_vector_moments(key, part):
    return moment_pair(key, 107, (LAYERS, 6, D), 0.8)


def raised(drawn, rng, source, target, shards_of, factor):
    def block_of(axis_at):
        return (jnp.arange(drawn.shape[axis_at]) // (drawn.shape[axis_at] // shards_of)).reshape((-1,) + (1,) * (drawn.ndim - 1 - axis_at))

    one_side = jax.random.permutation(rng, shards_of)[block_of(target)]
    other_side = (block_of(target) + shards_of // 2) % shards_of
    return jnp.where((block_of(source) == one_side) | (block_of(source) == other_side), factor * drawn, drawn)


def levels(rng, extent, cuts, low, top_value):
    level = 1.0
    for position, blocks in cuts:
        draws = jax.random.uniform(jax.random.fold_in(jax.random.fold_in(rng, 6), position), (blocks,), jnp.float32, low / len(cuts), top_value / len(cuts))
        level = level * jnp.repeat(jnp.exp(draws), extent[position] // blocks).reshape((-1,) + (1,) * (len(extent) - 1 - position))
    return level


def bell_draw(key, extent, deviation, bound, shards=(), kind=jnp.bfloat16):
    gain = levels(key, extent, shards, -0.22, 0.18) if shards else 1.0
    array = jax.random.normal(key, extent, jnp.float32) * deviation * gain
    return jnp.minimum(jnp.maximum(array, -bound), bound).astype(kind)


def heavy_noise(key, shape, deviation, most, cuts, heavy, held_as=jnp.bfloat16):
    array = deviation * jax.random.normal(key, shape, jnp.float32)
    if cuts:
        array = array * levels(key, shape, cuts, -0.22, 0.18)
    return jnp.clip(raised(array, jax.random.fold_in(key, 3), *heavy), -most, most).astype(held_as)


def setup_inputs(seed: int = 0) -> dict:
    seeds = jax.random.split(jax.random.key(seed), 17)
    return {
        "layer_input": draw_layer_input(jax.random.fold_in(seeds[16], 71), 0),
        "out_grad": heavy_noise(seeds[1], (TOKENS, D), 1.0, 6.0, ((0, 32),), (0, 1, 32, 2.75)),
        "qkv_weight": draw_qkv_weight(jax.random.fold_in(seeds[16], 71), 0),
        "qv_bias": bell_draw(seeds[3], (LAYERS, 2, D), 0.2, 0.8, ((2, 32),), jnp.float32),
        "proj_weight": bell_draw(seeds[4], (LAYERS, D, D), (max(12 * D // SEQ_LEN, 1)) ** -0.5, 1.0, ((1, 4), (2, 8)), jnp.float32),
        "up_weight": bell_draw(seeds[5], (LAYERS, D, FF), D ** -0.5, 0.21875, ((1, 8), (2, 4)), jnp.float32),
        "up_bias": bell_draw(seeds[6], (LAYERS, FF), 0.2, 0.8, ((1, 32),), jnp.float32),
        "down_weight": bell_draw(seeds[7], (LAYERS, FF, D), FF ** -0.5, 0.109375, ((1, 4), (2, 8)), jnp.float32),
        "norm_vectors": draw_norm_vectors(jax.random.fold_in(seeds[16], 71), 0),
        "qkv_moments": draw_qkv_moments(jax.random.fold_in(seeds[16], 71), 0),
        "qvbias_moments": draw_qvbias_moments(jax.random.fold_in(seeds[16], 71), 0),
        "proj_moments": draw_proj_moments(jax.random.fold_in(seeds[16], 71), 0),
        "up_moments": draw_up_moments(jax.random.fold_in(seeds[16], 71), 0),
        "upbias_moments": draw_upbias_moments(jax.random.fold_in(seeds[16], 71), 0),
        "down_moments": draw_down_moments(jax.random.fold_in(seeds[16], 71), 0),
        "vector_moments": draw_vector_moments(jax.random.fold_in(seeds[16], 71), 0),
    }


beta_one = 0.9
beta_two = 0.999
adam_eps = 1e-06
norm_eps = 1e-06
decay_matrix = 0.01
rate_matrix = 0.01
rate_output = 0.04
rate_vector = 0.15
root_half = 0.7071067811865476
inv_root_tau = 0.3989422804014327

def gelu_value(values):
    return 0.5 * values * (1.0 + lax.erf(values * root_half))

def gelu_slope(values):
    return 0.5 * (1.0 + lax.erf(values * root_half)) + values * jnp.exp(-0.5 * values * values) * inv_root_tau

def norm_forward(residual, gain_row, shift_row):
    center = residual - lax.optimization_barrier(jnp.mean(residual, axis=-1, keepdims=True))
    inv_std = lax.rsqrt(lax.optimization_barrier(jnp.mean(center * center, axis=-1, keepdims=True)) + norm_eps)
    normed = center * inv_std
    return (normed * gain_row + shift_row, normed, inv_std)

def norm_backward(incoming, normed, inv_std, gain_row):
    scaled = incoming * gain_row
    centered = scaled - lax.optimization_barrier(jnp.mean(scaled, axis=-1, keepdims=True)) - normed * lax.optimization_barrier(jnp.mean(scaled * normed, axis=-1, keepdims=True))
    return (inv_std * centered, lax.optimization_barrier(jnp.sum(incoming * normed, axis=0)), lax.optimization_barrier(jnp.sum(incoming, axis=0)))

def split_heads(flat_rows):
    return flat_rows.reshape(flat_rows.shape[0] // SEQ_LEN, SEQ_LEN, flat_rows.shape[1] // HEAD_DIM, HEAD_DIM)

def join_heads(split_rows):
    return split_rows.reshape(split_rows.shape[0] * split_rows.shape[1], split_rows.shape[2] * split_rows.shape[3])

def rounded_wide(values):
    return lax.optimization_barrier(values.astype(jnp.bfloat16)).astype(jnp.float32)

def product(left, right):
    return jnp.dot(left, right, preferred_element_type=jnp.float32)

def attend_forward(queries, key_rows, values):
    scaling = HEAD_DIM ** (-0.5)
    query_heads = split_heads(queries).astype(jnp.float32)
    key_heads = split_heads(key_rows).astype(jnp.float32)
    value_heads = split_heads(values).astype(jnp.float32)
    scores = jnp.einsum('sqhd,skhd->shqk', query_heads, key_heads) * scaling
    row_max = lax.optimization_barrier(jnp.max(scores, axis=-1, keepdims=True))
    log_total = row_max + jnp.log(lax.optimization_barrier(jnp.sum(jnp.exp(scores - row_max), axis=-1, keepdims=True)))
    probabilities = rounded_wide(jnp.exp(scores - log_total))
    result = jnp.einsum('shqk,skhd->sqhd', probabilities, value_heads)
    return (join_heads(result).astype(jnp.bfloat16), log_total)

def attend_backward(queries, key_rows, values, attended, log_total, grad_out):
    scaling = HEAD_DIM ** (-0.5)
    query_heads = split_heads(queries).astype(jnp.float32)
    key_heads = split_heads(key_rows).astype(jnp.float32)
    value_heads = split_heads(values).astype(jnp.float32)
    out_heads = split_heads(attended).astype(jnp.float32)
    grad_heads = split_heads(grad_out).astype(jnp.float32)
    scores = jnp.einsum('sqhd,skhd->shqk', query_heads, key_heads) * scaling
    probabilities = jnp.exp(scores - log_total)
    delta_row = jnp.einsum('sqhd,sqhd->shq', grad_heads, out_heads)[..., None]
    prob_grads = jnp.einsum('sqhd,skhd->shqk', grad_heads, value_heads)
    score_grads = rounded_wide(probabilities * (prob_grads - delta_row) * scaling)
    query_grad = jnp.einsum('shqk,skhd->sqhd', score_grads, key_heads)
    key_grad = jnp.einsum('shqk,sqhd->skhd', score_grads, query_heads)
    value_grad = jnp.einsum('shqk,sqhd->skhd', rounded_wide(probabilities), grad_heads)
    return (join_heads(query_grad).astype(jnp.bfloat16), join_heads(key_grad).astype(jnp.bfloat16), join_heads(value_grad).astype(jnp.bfloat16))

def round_layer(parameters, layer_at):
    return (parameters[0][layer_at].astype(jnp.bfloat16), rounded_wide(parameters[1][layer_at]), parameters[2][layer_at].astype(jnp.bfloat16), parameters[3][layer_at].astype(jnp.bfloat16), rounded_wide(parameters[4][layer_at]), parameters[5][layer_at].astype(jnp.bfloat16), rounded_wide(parameters[6][layer_at]))

def forward_layer(hidden, inputs, weights):
    w_qkv, b_qv, w_proj, w_up, b_up, w_down, vectors = weights
    queries = (product(inputs, w_qkv[0]) + b_qv[0]).astype(jnp.bfloat16)
    key_rows = product(inputs, w_qkv[1]).astype(jnp.bfloat16)
    values = (product(inputs, w_qkv[2]) + b_qv[1]).astype(jnp.bfloat16)
    attended, log_total = attend_forward(queries, key_rows, values)
    first_sum = hidden + product(attended, w_proj) + vectors[0]
    first_norm, normed_one, inv_one = norm_forward(first_sum, vectors[1], vectors[2])
    mid_inputs = first_norm.astype(jnp.bfloat16)
    pre_act = product(mid_inputs, w_up) + b_up
    activ = gelu_value(pre_act).astype(jnp.bfloat16)
    second_sum = first_norm + product(activ, w_down) + vectors[3]
    result, normed_two, inv_two = norm_forward(second_sum, vectors[4], vectors[5])
    stored = (inputs, queries, key_rows, values, attended, log_total, normed_one, inv_one, mid_inputs, pre_act, activ, normed_two, inv_two)
    return (result, stored)

def backward_layer(incoming, stored, weights):
    inputs, queries, key_rows, values, attended, log_total, normed_one, inv_one, mid_inputs, pre_act, activ, normed_two, inv_two = stored
    w_qkv, b_qv, w_proj, w_up, b_up, w_down, vectors = weights
    second_grad, gain_two, shift_two = norm_backward(incoming, normed_two, inv_two, vectors[4])
    sent_two = second_grad.astype(jnp.bfloat16)
    down_grad = product(activ.T, sent_two)
    act_grad = product(sent_two, w_down.T) * gelu_slope(pre_act)
    upbias_grad = lax.optimization_barrier(jnp.sum(act_grad, axis=0))
    act_sent = act_grad.astype(jnp.bfloat16)
    up_grad = product(mid_inputs.T, act_sent)
    mid_grad = second_grad + product(act_sent, w_up.T)
    first_grad, gain_one, shift_one = norm_backward(mid_grad, normed_one, inv_one, vectors[1])
    sent_one = first_grad.astype(jnp.bfloat16)
    proj_grad = product(attended.T, sent_one)
    attended_grad = product(sent_one, w_proj.T).astype(jnp.bfloat16)
    query_grad, key_grad, value_grad = attend_backward(queries, key_rows, values, attended, log_total, attended_grad)
    qkv_grad = jnp.stack([product(inputs.T, query_grad), product(inputs.T, key_grad), product(inputs.T, value_grad)])
    qvbias_grad = jnp.stack([lax.optimization_barrier(jnp.sum(query_grad, axis=0, dtype=jnp.float32)), lax.optimization_barrier(jnp.sum(value_grad, axis=0, dtype=jnp.float32))])
    input_grad = first_grad + product(query_grad, w_qkv[0].T) + product(key_grad, w_qkv[1].T) + product(value_grad, w_qkv[2].T)
    vector_grad = jnp.stack([lax.optimization_barrier(jnp.sum(first_grad, axis=0)), gain_one, shift_one, lax.optimization_barrier(jnp.sum(second_grad, axis=0)), gain_two, shift_two])
    return (input_grad, (qkv_grad, qvbias_grad, proj_grad, up_grad, upbias_grad, down_grad, vector_grad))

def adam_update(parameter, gradient, moments, learn_rate, decay_rate):
    first_mom = beta_one * moments[0] + (1.0 - beta_one) * gradient
    second_mom = beta_two * moments[1] + (1.0 - beta_two) * gradient * gradient
    direction = first_mom / (1.0 - beta_one ** ADAM_STEP) / (jnp.sqrt(second_mom / (1.0 - beta_two ** ADAM_STEP)) + adam_eps)
    return (parameter - learn_rate * (direction + decay_rate * parameter), jnp.stack([first_mom, second_mom]))

def reference(layer_input, out_grad, qkv_weight, qv_bias, proj_weight, up_weight, up_bias, down_weight, norm_vectors, qkv_moments, qvbias_moments, proj_moments, up_moments, upbias_moments, down_moments, vector_moments):
    parameters = (qkv_weight, qv_bias, proj_weight, up_weight, up_bias, down_weight, norm_vectors)
    moment_list = (qkv_moments, qvbias_moments, proj_moments, up_moments, upbias_moments, down_moments, vector_moments)
    weights = [round_layer(parameters, layer_at) for layer_at in range(LAYERS)]
    block_rows = SEQ_DP * SEQ_LEN
    input_blocks = layer_input.reshape(N_DP, block_rows, D)
    grad_blocks = out_grad.reshape(N_DP, block_rows, D)
    zeros = tuple((jnp.zeros(parameter.shape, jnp.float32) for parameter in parameters))

    def block_step(totals, block_pair):
        block_in, block_grad = block_pair
        hidden = block_in.astype(jnp.float32)
        inputs = block_in
        stored_all = []
        for layer_at in range(LAYERS):
            if layer_at > 0:
                inputs = hidden.astype(jnp.bfloat16)
            hidden, stored = forward_layer(hidden, inputs, weights[layer_at])
            stored_all.append(stored)
        output_rows = hidden.astype(jnp.bfloat16)
        incoming = block_grad.astype(jnp.float32)
        layer_grads = [None] * LAYERS
        for layer_at in reversed(range(LAYERS)):
            incoming, layer_grads[layer_at] = backward_layer(incoming, stored_all[layer_at], weights[layer_at])
        stacked = tuple((jnp.stack([entry[member] for entry in layer_grads]) for member in range(7)))
        totals = tuple((total + extra for total, extra in zip(totals, stacked)))
        return (totals, (output_rows, incoming))
    totals, (output_blocks, input_grads) = lax.scan(block_step, zeros, (input_blocks, grad_blocks))
    rates = (rate_matrix, rate_vector, rate_output, rate_matrix, rate_vector, rate_matrix, rate_vector)
    decays = (decay_matrix, 0.0, decay_matrix, decay_matrix, 0.0, decay_matrix, 0.0)
    results = [adam_update(parameters[member], totals[member], moment_list[member], rates[member], decays[member]) for member in range(7)]
    return (output_blocks.reshape(TOKENS, D), input_grads.reshape(TOKENS, D), totals[0], totals[1], totals[2], totals[3], totals[4], totals[5], totals[6], results[0][0], results[1][0], results[2][0], results[3][0], results[4][0], results[5][0], results[6][0], results[0][1], results[1][1], results[2][1], results[3][1], results[4][1], results[5][1], results[6][1])
```

```python
import jax
import jax.numpy as jnp
from jax import lax
from jax.sharding import PartitionSpec as P

HEAD_DIM = 64
SEQ_LEN = 256
ADAM_STEP = 3


beta_one = 0.9
beta_two = 0.999
adam_eps = 1e-06
norm_eps = 1e-06
decay_matrix = 0.01
rate_matrix = 0.01
rate_output = 0.04
rate_vector = 0.15
root_half = 0.7071067811865476
inv_root_tau = 0.3989422804014327

bf16 = jnp.bfloat16
f32 = jnp.float32


def gelu_value(values):
    return 0.5 * values * (1.0 + lax.erf(values * root_half))


def gelu_slope(values):
    return (
        0.5 * (1.0 + lax.erf(values * root_half))
        + values * jnp.exp(-0.5 * values * values) * inv_root_tau
    )


def norm_forward(residual, gain_row, shift_row):
    center = residual - jnp.mean(residual, axis=-1, keepdims=True)
    inv_std = lax.rsqrt(jnp.mean(center * center, axis=-1, keepdims=True) + norm_eps)
    normed = center * inv_std
    return (normed * gain_row + shift_row, normed, inv_std)


def norm_backward(incoming, normed, inv_std, gain_row):
    scaled = incoming * gain_row
    centered = (
        scaled
        - jnp.mean(scaled, axis=-1, keepdims=True)
        - normed * jnp.mean(scaled * normed, axis=-1, keepdims=True)
    )
    return (inv_std * centered, jnp.sum(incoming * normed, axis=0), jnp.sum(incoming, axis=0))


def split_heads(flat_rows):
    return flat_rows.reshape(
        flat_rows.shape[0] // SEQ_LEN, SEQ_LEN, flat_rows.shape[1] // HEAD_DIM, HEAD_DIM
    )


def join_heads(split_rows):
    return split_rows.reshape(
        split_rows.shape[0] * split_rows.shape[1], split_rows.shape[2] * split_rows.shape[3]
    )


def product(left, right):
    return jnp.dot(left, right, preferred_element_type=f32)


def contract_rows(left, right):
    return lax.dot_general(left, right, (((0,), (0,)), ((), ())), preferred_element_type=f32)


def times_transpose(left, right):
    return lax.dot_general(left, right, (((1,), (1,)), ((), ())), preferred_element_type=f32)


def attend_forward(queries, key_rows, values):
    scaling = HEAD_DIM ** (-0.5)
    scores = (
        jnp.einsum(
            "sqhd,skhd->shqk",
            split_heads(queries),
            split_heads(key_rows),
            preferred_element_type=f32,
        )
        * scaling
    )
    row_max = jnp.max(scores, axis=-1, keepdims=True)
    log_total = row_max + jnp.log(jnp.sum(jnp.exp(scores - row_max), axis=-1, keepdims=True))
    probabilities = jnp.exp(scores - log_total).astype(bf16)
    result = jnp.einsum(
        "shqk,skhd->sqhd", probabilities, split_heads(values), preferred_element_type=f32
    )
    return (join_heads(result).astype(bf16), log_total)


def attend_backward(queries, key_rows, values, attended, log_total, grad_out):
    scaling = HEAD_DIM ** (-0.5)
    query_heads = split_heads(queries)
    key_heads = split_heads(key_rows)
    value_heads = split_heads(values)
    out_heads = split_heads(attended)
    grad_heads = split_heads(grad_out)
    scores = (
        jnp.einsum("sqhd,skhd->shqk", query_heads, key_heads, preferred_element_type=f32) * scaling
    )
    probabilities = jnp.exp(scores - log_total)
    delta_row = jnp.einsum("sqhd,sqhd->shq", grad_heads, out_heads, preferred_element_type=f32)[
        ..., None
    ]
    prob_grads = jnp.einsum("sqhd,skhd->shqk", grad_heads, value_heads, preferred_element_type=f32)
    score_grads = (probabilities * (prob_grads - delta_row) * scaling).astype(bf16)
    query_grad = jnp.einsum("shqk,skhd->sqhd", score_grads, key_heads, preferred_element_type=f32)
    key_grad = jnp.einsum("shqk,sqhd->skhd", score_grads, query_heads, preferred_element_type=f32)
    value_grad = jnp.einsum(
        "shqk,sqhd->skhd", probabilities.astype(bf16), grad_heads, preferred_element_type=f32
    )
    return (
        join_heads(query_grad).astype(bf16),
        join_heads(key_grad).astype(bf16),
        join_heads(value_grad).astype(bf16),
    )


def swap_dp(value, mask):
    size = lax.axis_size("dp")
    return lax.ppermute(value, "dp", [(at, at ^ mask) for at in range(size)])


def swap_tensor(value, mask):
    size = lax.axis_size("tensor")
    return lax.ppermute(value, "tensor", [(at, at ^ mask) for at in range(size)])


def gather_far(block):
    size = lax.axis_size("dp")
    return [block] + [swap_dp(block, mask) for mask in range(2, size, 2)]


def gather_matrix(block):
    far = gather_far(block)
    half = len(far) // 2
    one = jnp.concatenate(far[:half])
    two = jnp.concatenate(far[half:])
    one_x = swap_dp(one, 1)
    two_y = swap_tensor(two, 2)
    one_y = swap_tensor(one, 2)
    two_x = swap_dp(two, 1)
    one_xy = swap_tensor(one_x, 2)
    two_xy = swap_dp(two_y, 1)
    own = jnp.concatenate([one, two, one_x, two_x])
    other = jnp.concatenate([one_y, two_y, one_xy, two_xy])
    return own, other


def add_pair(left, right):
    return (left.astype(f32) + right.astype(f32)).astype(bf16)


def reduce_matrix(own, other):
    quarter = own.shape[0] // 4
    one, two, one_x, two_x = (own[at * quarter : (at + 1) * quarter] for at in range(4))
    one_y, two_y, one_xy, two_xy = (other[at * quarter : (at + 1) * quarter] for at in range(4))
    one_x = add_pair(one_x, swap_tensor(one_xy, 2))
    two_y = add_pair(two_y, swap_dp(two_xy, 1))
    one = add_pair(one, swap_tensor(one_y, 2))
    two = add_pair(two, swap_dp(two_x, 1))
    one = add_pair(one, swap_dp(one_x, 1))
    two = add_pair(two, swap_tensor(two_y, 2))
    half = lax.axis_size("dp") // 4
    rows = quarter // half
    total = one[:rows].astype(f32)
    for at in range(1, 2 * half):
        source = one if at < half else two
        start = (at % half) * rows
        total = total + swap_dp(source[start : start + rows], 2 * at).astype(f32)
    return total


def reduce_pair(partial):
    rows = partial.shape[0] // 2
    return partial[:rows] + swap_tensor(partial[rows:].astype(bf16), 1).astype(f32)


def gather_pair(rows):
    return jnp.concatenate([rows, swap_tensor(rows, 1)])


def block_masks():
    half = lax.axis_size("dp") // 2
    return [(at % half) * 2 + at // half for at in range(2 * half)]


def mask_row():
    size = lax.axis_size("dp")
    half = size // 2
    at = lax.broadcasted_iota(jnp.int32, (1, size), 1)
    return lax.bitwise_xor(lax.axis_index("dp"), (at % half) * 2 + at // half)


def block_selector():
    size = lax.axis_size("dp")
    return lax.broadcasted_iota(jnp.int32, (size, size), 0) == mask_row()


def column_selector(width, block):
    half = lax.axis_size("dp") // 2
    column = lax.broadcasted_iota(jnp.int32, (1, width), 1)
    at = column // block
    actual = lax.bitwise_xor(lax.axis_index("dp"), (at % half) * 2 + at // half) * block + (
        column % block
    )
    return lax.broadcasted_iota(jnp.int32, (width, width), 0) == actual


def forward_layer(hidden, weights, small):
    mix, rise, fall = weights
    b_q, b_v, b_up, vectors = small
    head = b_q[0].shape[0]
    inputs = gather_pair(hidden.astype(bf16))
    queries, key_rows, values = [], [], []
    for side in range(2):
        projected = product(inputs, mix[side])
        queries.append((projected[:, :head] + b_q[side]).astype(bf16))
        key_rows.append(projected[:, head : 2 * head].astype(bf16))
        values.append((projected[:, 2 * head : 3 * head] + b_v[side]).astype(bf16))
    queries, key_rows, values = (
        jnp.concatenate(entry, axis=1) for entry in (queries, key_rows, values)
    )
    attended, log_total = attend_forward(queries, key_rows, values)
    partial = times_transpose(attended[:, :head], mix[0][:, 3 * head :]) + times_transpose(
        attended[:, head:], mix[1][:, 3 * head :]
    )
    first_sum = hidden + reduce_pair(partial) + vectors[0]
    first_norm, normed_one, inv_one = norm_forward(first_sum, vectors[1], vectors[2])
    mid_inputs = gather_pair(first_norm.astype(bf16))
    pre_act = [product(mid_inputs, rise[side]) + b_up[side] for side in range(2)]
    activ = [gelu_value(entry).astype(bf16) for entry in pre_act]
    partial = times_transpose(activ[0], fall[0]) + times_transpose(activ[1], fall[1])
    second_sum = first_norm + reduce_pair(partial) + vectors[3]
    result, normed_two, inv_two = norm_forward(second_sum, vectors[4], vectors[5])
    stored = (
        inputs,
        queries,
        key_rows,
        values,
        attended,
        log_total,
        normed_one,
        inv_one,
        mid_inputs,
        pre_act,
        activ,
        normed_two,
        inv_two,
    )
    return (result, stored)


def backward_layer(incoming, stored, weights, small):
    (
        inputs,
        queries,
        key_rows,
        values,
        attended,
        log_total,
        normed_one,
        inv_one,
        mid_inputs,
        pre_act,
        activ,
        normed_two,
        inv_two,
    ) = stored
    mix, rise, fall = weights
    vectors = small[3]
    head = small[0][0].shape[0]
    second_grad, gain_two, shift_two = norm_backward(incoming, normed_two, inv_two, vectors[4])
    sent_two = gather_pair(second_grad.astype(bf16))
    fall_grad = reduce_matrix(
        *(contract_rows(sent_two, activ[side]).astype(bf16) for side in range(2))
    )
    act_grad = [product(sent_two, fall[side]) * gelu_slope(pre_act[side]) for side in range(2)]
    act_sent = [entry.astype(bf16) for entry in act_grad]
    rise_grad = reduce_matrix(
        *(contract_rows(mid_inputs, act_sent[side]).astype(bf16) for side in range(2))
    )
    partial = times_transpose(act_sent[0], rise[0]) + times_transpose(act_sent[1], rise[1])
    mid_grad = second_grad + reduce_pair(partial)
    first_grad, gain_one, shift_one = norm_backward(mid_grad, normed_one, inv_one, vectors[1])
    sent_one = gather_pair(first_grad.astype(bf16))
    attended_grad = jnp.concatenate(
        [product(sent_one, mix[side][:, 3 * head :]).astype(bf16) for side in range(2)], axis=1
    )
    query_grad, key_grad, value_grad = attend_backward(
        queries, key_rows, values, attended, log_total, attended_grad
    )
    sides = [slice(0, head), slice(head, 2 * head)]
    stacked = [
        jnp.concatenate([query_grad[:, at], key_grad[:, at], value_grad[:, at]], axis=1)
        for at in sides
    ]
    mix_grad = reduce_matrix(
        *(
            jnp.concatenate(
                [
                    contract_rows(inputs, stacked[side]),
                    contract_rows(sent_one, attended[:, sides[side]]),
                ],
                axis=1,
            ).astype(bf16)
            for side in range(2)
        )
    )
    partial = times_transpose(stacked[0], mix[0][:, : 3 * head]) + times_transpose(
        stacked[1], mix[1][:, : 3 * head]
    )
    input_grad = first_grad + reduce_pair(partial)
    vector_grad = jnp.stack(
        [
            jnp.sum(first_grad, axis=0),
            gain_one,
            shift_one,
            jnp.sum(second_grad, axis=0),
            gain_two,
            shift_two,
        ]
    )
    query_sum = jnp.sum(query_grad, axis=0, dtype=f32)
    value_sum = jnp.sum(value_grad, axis=0, dtype=f32)
    bias_grad = [
        (query_sum[sides[side]], value_sum[sides[side]], jnp.sum(act_grad[side], axis=0))
        for side in range(2)
    ]
    return (input_grad, (mix_grad, rise_grad, fall_grad), vector_grad, bias_grad)


def adam_update(parameter, gradient, moments, learn_rate, decay_rate):
    first_mom = beta_one * moments[0] + (1.0 - beta_one) * gradient
    second_mom = beta_two * moments[1] + (1.0 - beta_two) * gradient * gradient
    direction = (
        first_mom
        / (1.0 - beta_one**ADAM_STEP)
        / (jnp.sqrt(second_mom / (1.0 - beta_two**ADAM_STEP)) + adam_eps)
    )
    return (
        parameter - learn_rate * (direction + decay_rate * parameter),
        jnp.stack([first_mom, second_mom]),
    )


def pack_mix(qkv, proj):
    parts = [qkv[at] for at in range(qkv.shape[0])] + [proj.T]
    return jnp.concatenate(parts, axis=1).astype(bf16)


def gather_small(qv_bias, up_bias, norm_vectors):
    layers, _, block = norm_vectors.shape
    size = lax.axis_size("dp")
    width = qv_bias.shape[2]
    packed = jnp.concatenate(
        [norm_vectors.reshape(1, -1), up_bias.reshape(1, -1), qv_bias.reshape(1, -1)], axis=1
    ).astype(bf16)
    near = jnp.concatenate(gather_far(packed))
    own = jnp.concatenate([near, swap_dp(near, 1)])
    rank = norm_vectors.size
    other = swap_tensor(own[:, rank:], 2)
    vectors = (
        own[:, :rank].reshape(size, layers, 6, block).transpose(1, 2, 0, 3).reshape(layers, 6, -1)
    ).astype(f32)
    selector = block_selector().astype(bf16)
    ups, queries, values = [], [], []
    for entry in (own[:, rank:], other):
        entry = product(selector, entry)
        up = entry[:, : up_bias.size].reshape(size, layers, block)
        ups.append(up.transpose(1, 0, 2).reshape(layers, -1))
        qv = entry[:, up_bias.size :].reshape(size, layers, 2, width)
        qv = qv.transpose(1, 2, 0, 3).reshape(layers, 2, -1)
        queries.append(qv[:, 0])
        values.append(qv[:, 1])
    return [
        (
            [entry[at] for entry in queries],
            [entry[at] for entry in values],
            [entry[at] for entry in ups],
            vectors[at],
        )
        for at in range(layers)
    ]


def reduce_small(vector_grads, bias_grads, block, width):
    size = lax.axis_size("dp")
    layers = len(vector_grads)
    vectors = jnp.stack(vector_grads)
    vectors = vectors.reshape(layers * 6, size, block).transpose(1, 0, 2).reshape(size, -1)
    sides = []
    for side in range(2):
        parts = []
        for at in range(layers):
            query_sum, value_sum, up_sum = bias_grads[at][side]
            parts += [
                query_sum.reshape(size, width),
                value_sum.reshape(size, width),
                up_sum.reshape(size, block),
            ]
        sides.append(jnp.concatenate(parts, axis=1))
    selector = block_selector().astype(f32)
    placed = lax.dot_general(
        selector,
        jnp.concatenate(sides, axis=1),
        (((0,), (0,)), ((), ())),
        precision=lax.Precision.HIGHEST,
        preferred_element_type=f32,
    )
    span = sides[0].shape[1]
    vectors = vectors + swap_tensor(vectors, 1)
    received = swap_tensor(jnp.concatenate([vectors, placed[:, span:]], axis=1), 2)
    total = jnp.concatenate([vectors, placed[:, :span]], axis=1) + received
    half = size // 2
    total = total[:half] + swap_dp(total[half:], 1)
    result = total[0:1]
    for at in range(1, half):
        result = result + swap_dp(total[at : at + 1], 2 * at)
    result = result[0]
    rank = layers * 6 * block
    vector_grad = result[:rank].reshape(layers, 6, block)
    rest = result[rank:].reshape(layers, -1)
    qv_grad = rest[:, : 2 * width].reshape(layers, 2, width)
    return vector_grad, qv_grad, rest[:, 2 * width :]


def on_device(
    layer_input,
    out_grad,
    qkv_weight,
    qv_bias,
    proj_weight,
    up_weight,
    up_bias,
    down_weight,
    norm_vectors,
    qkv_moments,
    qvbias_moments,
    proj_moments,
    up_moments,
    upbias_moments,
    down_moments,
    vector_moments,
):
    layers = qkv_weight.shape[0]
    block = norm_vectors.shape[2]
    width = qv_bias.shape[2]
    small = gather_small(qv_bias, up_bias, norm_vectors)
    weights = []
    for at in range(layers):
        weights.append(
            (
                gather_matrix(pack_mix(qkv_weight[at], proj_weight[at])),
                gather_matrix(up_weight[at].astype(bf16)),
                gather_matrix(down_weight[at].T.astype(bf16)),
            )
        )
    rows, model = layer_input.shape
    selector = column_selector(model, block).astype(bf16)
    ordered = product(jnp.concatenate([layer_input, out_grad]), selector)
    hidden, incoming = ordered[:rows], ordered[rows:]
    stored_all = []
    for at in range(layers):
        hidden, stored = forward_layer(hidden, weights[at], small[at])
        stored_all.append(stored)
    block_output = times_transpose(hidden.astype(bf16), selector).astype(bf16)
    reduced = [None] * layers
    vector_grads = [None] * layers
    bias_grads = [None] * layers
    for at in reversed(range(layers)):
        incoming, reduced[at], vector_grads[at], bias_grads[at] = backward_layer(
            incoming, stored_all[at], weights[at], small[at]
        )
    input_grad = lax.dot_general(
        incoming,
        selector.astype(f32),
        (((1,), (1,)), ((), ())),
        precision=lax.Precision.HIGHEST,
        preferred_element_type=f32,
    )
    vector_grad, qv_grad, up_bias_grad = reduce_small(vector_grads, bias_grads, block, width)
    head = qkv_weight.shape[3]
    qkv_grad = jnp.stack(
        [
            jnp.stack([entry[0][:, at * head : (at + 1) * head] for at in range(3)])
            for entry in reduced
        ]
    )
    proj_grad = jnp.stack([entry[0][:, 3 * head :].T for entry in reduced])
    up_grad = jnp.stack([entry[1] for entry in reduced])
    down_grad = jnp.stack([entry[2].T for entry in reduced])
    gradients = (qkv_grad, qv_grad, proj_grad, up_grad, up_bias_grad, down_grad, vector_grad)
    parameters = (qkv_weight, qv_bias, proj_weight, up_weight, up_bias, down_weight, norm_vectors)
    moment_list = (
        qkv_moments,
        qvbias_moments,
        proj_moments,
        up_moments,
        upbias_moments,
        down_moments,
        vector_moments,
    )
    rates = (
        rate_matrix,
        rate_vector,
        rate_output,
        rate_matrix,
        rate_vector,
        rate_matrix,
        rate_vector,
    )
    decays = (decay_matrix, 0.0, decay_matrix, decay_matrix, 0.0, decay_matrix, 0.0)
    results = [
        adam_update(
            parameters[member],
            gradients[member],
            moment_list[member],
            rates[member],
            decays[member],
        )
        for member in range(7)
    ]
    return (
        block_output,
        input_grad,
        *gradients,
        *(entry[0] for entry in results),
        *(entry[1] for entry in results),
    )


def solution(mesh):
    return jax.shard_map(
        on_device,
        mesh=mesh,
        in_specs=(
            P(("dp", "tensor"), None),
            P(("dp", "tensor"), None),
            P(None, None, "dp", "tensor"),
            P(None, None, ("tensor", "dp")),
            P(None, "tensor", "dp"),
            P(None, "dp", "tensor"),
            P(None, ("tensor", "dp")),
            P(None, "tensor", "dp"),
            P(None, None, "dp"),
            P(None, None, None, "dp", "tensor"),
            P(None, None, None, ("tensor", "dp")),
            P(None, None, "tensor", "dp"),
            P(None, None, "dp", "tensor"),
            P(None, None, ("tensor", "dp")),
            P(None, None, "tensor", "dp"),
            P(None, None, None, "dp"),
        ),
        out_specs=(
            P(("dp", "tensor"), None),
            P(("dp", "tensor"), None),
            P(None, None, "dp", "tensor"),
            P(None, None, ("tensor", "dp")),
            P(None, "tensor", "dp"),
            P(None, "dp", "tensor"),
            P(None, ("tensor", "dp")),
            P(None, "tensor", "dp"),
            P(None, None, "dp"),
            P(None, None, "dp", "tensor"),
            P(None, None, ("tensor", "dp")),
            P(None, "tensor", "dp"),
            P(None, "dp", "tensor"),
            P(None, ("tensor", "dp")),
            P(None, "tensor", "dp"),
            P(None, None, "dp"),
            P(None, None, None, "dp", "tensor"),
            P(None, None, None, ("tensor", "dp")),
            P(None, None, "tensor", "dp"),
            P(None, None, "dp", "tensor"),
            P(None, None, ("tensor", "dp")),
            P(None, None, "tensor", "dp"),
            P(None, None, None, "dp"),
        ),
        check_vma=False,
    )
```

```python
import jax
import jax.numpy as jnp
from jax import lax
from jax.experimental import pallas as pl
from jax.experimental.pallas import tpu as pltpu
from jax.sharding import PartitionSpec as P

HEAD_DIM = 64
SEQ_LEN = 256
ADAM_STEP = 3


beta_one = 0.9
beta_two = 0.999
adam_eps = 1e-06
norm_eps = 1e-06
decay_matrix = 0.01
rate_matrix = 0.01
rate_output = 0.04
rate_vector = 0.15
root_half = 0.7071067811865476
inv_root_tau = 0.3989422804014327

bf16 = jnp.bfloat16
f32 = jnp.float32


def gelu_value(values):
    return 0.5 * values * (1.0 + lax.erf(values * root_half))


def gelu_slope(values):
    return (
        0.5 * (1.0 + lax.erf(values * root_half))
        + values * jnp.exp(-0.5 * values * values) * inv_root_tau
    )


def norm_forward(residual, gain_row, shift_row):
    center = residual - jnp.mean(residual, axis=-1, keepdims=True)
    inv_std = lax.rsqrt(jnp.mean(center * center, axis=-1, keepdims=True) + norm_eps)
    normed = center * inv_std
    return (normed * gain_row + shift_row, normed, inv_std)


def norm_backward(incoming, normed, inv_std, gain_row):
    scaled = incoming * gain_row
    centered = (
        scaled
        - jnp.mean(scaled, axis=-1, keepdims=True)
        - normed * jnp.mean(scaled * normed, axis=-1, keepdims=True)
    )
    return (inv_std * centered, jnp.sum(incoming * normed, axis=0), jnp.sum(incoming, axis=0))


def contract(left, right, dims):
    return lax.dot_general(left, right, ((dims[:1], dims[1:]), ((), ())), preferred_element_type=f32)


def shape(rows, columns, dtype):
    return jax.ShapeDtypeStruct((rows, columns), dtype)


def run_kernel(body, outs, scratch, flops, *operands):
    moved = sum(entry.size * entry.dtype.itemsize for entry in (*operands, *outs))
    place = pl.BlockSpec(memory_space=pltpu.VMEM)
    return pl.pallas_call(
        body,
        out_shape=tuple(outs),
        in_specs=[place] * len(operands),
        out_specs=tuple([place] * len(outs)),
        scratch_shapes=scratch,
        cost_estimate=pl.CostEstimate(flops=flops, bytes_accessed=moved, transcendentals=0),
    )(*operands)


def join_rows(first_ref, second_ref):
    return jnp.concatenate([first_ref[...], second_ref[...]], axis=0)


def fill(target_ref, pieces, start, size):
    for at, piece in enumerate(pieces):
        target_ref[at * size : (at + 1) * size, :] = piece[start : start + size, :]


def put_partial(partial, own_ref, send_ref):
    rows = own_ref.shape[0]
    own_ref[...] = partial[:rows]
    send_ref[...] = partial[rows:].astype(bf16)


def attend_forward_body(own_ref, recv_ref, bias_ref, *refs):
    pieces, (side_a, side_b, log_ref, part_ref, send_ref, w_ref) = refs[:8], refs[8:]
    size = pieces[0].shape[0]
    head = w_ref.shape[1] // 4
    scaling = HEAD_DIM ** (-0.5)
    inputs = join_rows(own_ref, recv_ref)
    partial = None
    for side, out_ref in enumerate((side_a, side_b)):
        fill(w_ref, pieces[4 * side : 4 * side + 4], 0, size)
        mixed = jnp.dot(inputs, w_ref[...], preferred_element_type=f32)
        mixed = (mixed + bias_ref[side : side + 1, :]).astype(bf16)
        out_ref[...] = mixed
        found = []
        for at in range(head // HEAD_DIM):
            start = at * HEAD_DIM
            query = mixed[:, start : start + HEAD_DIM]
            key = mixed[:, head + start : head + start + HEAD_DIM]
            value = mixed[:, 2 * head + start : 2 * head + start + HEAD_DIM]
            scores = contract(query, key, (1, 1)) * scaling
            row_max = jnp.max(scores, axis=-1, keepdims=True)
            raised = jnp.exp(scores - row_max)
            total = jnp.sum(raised, axis=-1, keepdims=True)
            column = side * (head // HEAD_DIM) + at
            log_ref[:, column : column + 1] = row_max + jnp.log(total)
            probabilities = (raised * (1.0 / total)).astype(bf16)
            found.append(jnp.dot(probabilities, value, preferred_element_type=f32))
        attended = jnp.concatenate(found, axis=1).astype(bf16)
        out_ref[:, 3 * head :] = attended
        term = contract(attended, w_ref[:, 3 * head :], (1, 1))
        partial = term if partial is None else partial + term
    put_partial(partial, part_ref, send_ref)


def attend_backward_body(own_ref, recv_ref, side_a, side_b, log_ref, *refs):
    pieces, (grad_a, grad_b, sum_ref, part_ref, send_ref, w_ref) = refs[:8], refs[8:]
    size = pieces[0].shape[0]
    head = w_ref.shape[1] // 4
    scaling = HEAD_DIM ** (-0.5)
    incoming = join_rows(own_ref, recv_ref)
    partial = None
    for side, (in_ref, out_ref) in enumerate(((side_a, grad_a), (side_b, grad_b))):
        fill(w_ref, pieces[4 * side : 4 * side + 4], 0, size)
        mixed = in_ref[...]
        spread = jnp.dot(incoming, w_ref[:, 3 * head :], preferred_element_type=f32).astype(bf16)
        grads = [[], [], []]
        for at in range(head // HEAD_DIM):
            start = at * HEAD_DIM
            query = mixed[:, start : start + HEAD_DIM]
            key = mixed[:, head + start : head + start + HEAD_DIM]
            value = mixed[:, 2 * head + start : 2 * head + start + HEAD_DIM]
            attended = mixed[:, 3 * head + start : 3 * head + start + HEAD_DIM]
            grad = spread[:, start : start + HEAD_DIM]
            column = side * (head // HEAD_DIM) + at
            scores = contract(query, key, (1, 1)) * scaling
            probabilities = jnp.exp(scores - log_ref[:, column : column + 1])
            delta = jnp.sum(grad.astype(f32) * attended.astype(f32), axis=-1, keepdims=True)
            prob_grads = contract(grad, value, (1, 1))
            score_grads = (probabilities * (prob_grads - delta) * scaling).astype(bf16)
            grads[0].append(jnp.dot(score_grads, key, preferred_element_type=f32))
            grads[1].append(contract(score_grads, query, (0, 0)))
            grads[2].append(contract(probabilities.astype(bf16), grad, (0, 0)))
        parts = [jnp.concatenate(entry, axis=1) for entry in grads]
        joined = jnp.concatenate(parts + [jnp.zeros_like(parts[0])], axis=1).astype(bf16)
        out_ref[...] = joined
        sum_ref[side : side + 1, :] = jnp.sum(joined.astype(f32), axis=0, keepdims=True)
        term = contract(joined, w_ref[...], (1, 1))
        partial = term if partial is None else partial + term
    put_partial(partial, part_ref, send_ref)


def mix_grad_body(own_ref, recv_ref, cot_own_ref, cot_recv_ref, grad_a, grad_b, side_a, side_b, *outs):
    inputs = join_rows(own_ref, recv_ref).T
    cotangents = join_rows(cot_own_ref, cot_recv_ref).T
    size = outs[0].shape[0]
    head = grad_a.shape[1] // 4
    for side, (grad_ref, side_ref) in enumerate(((grad_a, side_a), (grad_b, side_b))):
        for at in range(4):
            out_ref = outs[4 * side + at]
            rows = slice(at * size, (at + 1) * size)
            out_ref[...] = jnp.dot(
                inputs[rows], grad_ref[...], preferred_element_type=f32
            ).astype(bf16)
            out_ref[:, 3 * head :] = jnp.dot(
                cotangents[rows], side_ref[:, 3 * head :], preferred_element_type=f32
            ).astype(bf16)


def hidden_forward_body(own_ref, recv_ref, bias_ref, *refs):
    pieces, (slope_a, slope_b, act_a, act_b, part_ref, send_ref, w_ref) = refs[:8], refs[8:]
    size = pieces[0].shape[0] // 2
    inputs = join_rows(own_ref, recv_ref)
    partial = None
    for side, (slope_ref, act_ref) in enumerate(((slope_a, act_a), (slope_b, act_b))):
        mine = pieces[4 * side : 4 * side + 4]
        fill(w_ref, mine, 0, size)
        values = jnp.dot(inputs, w_ref[...], preferred_element_type=f32)
        values = values + bias_ref[side : side + 1, :]
        gate = 0.5 * (1.0 + lax.erf(values * root_half))
        slope_ref[...] = gate + values * jnp.exp(-0.5 * values * values) * inv_root_tau
        act_ref[...] = (values * gate).astype(bf16)
        fill(w_ref, mine, size, size)
        term = contract(act_ref[...], w_ref[...], (1, 1))
        partial = term if partial is None else partial + term
    put_partial(partial, part_ref, send_ref)


def hidden_backward_body(own_ref, recv_ref, slope_a, slope_b, *refs):
    pieces, (grad_a, grad_b, sum_ref, part_ref, send_ref, w_ref) = refs[:8], refs[8:]
    size = pieces[0].shape[0] // 2
    incoming = join_rows(own_ref, recv_ref)
    partial = None
    for side, (slope_ref, grad_ref) in enumerate(((slope_a, grad_a), (slope_b, grad_b))):
        mine = pieces[4 * side : 4 * side + 4]
        fill(w_ref, mine, size, size)
        grad = jnp.dot(incoming, w_ref[...], preferred_element_type=f32) * slope_ref[...]
        sum_ref[side : side + 1, :] = jnp.sum(grad, axis=0, keepdims=True)
        grad_ref[...] = grad.astype(bf16)
        fill(w_ref, mine, 0, size)
        term = contract(grad_ref[...], w_ref[...], (1, 1))
        partial = term if partial is None else partial + term
    put_partial(partial, part_ref, send_ref)


def hidden_grad_body(own_ref, recv_ref, cot_own_ref, cot_recv_ref, grad_a, grad_b, act_a, act_b, *outs):
    inputs = join_rows(own_ref, recv_ref).T
    cotangents = join_rows(cot_own_ref, cot_recv_ref).T
    size = outs[0].shape[0] // 2
    for side, (grad_ref, act_ref) in enumerate(((grad_a, act_a), (grad_b, act_b))):
        for at in range(4):
            out_ref = outs[4 * side + at]
            rows = slice(at * size, (at + 1) * size)
            out_ref[:size, :] = jnp.dot(
                inputs[rows], grad_ref[...], preferred_element_type=f32
            ).astype(bf16)
            out_ref[size:, :] = jnp.dot(
                cotangents[rows], act_ref[...], preferred_element_type=f32
            ).astype(bf16)


def norm_forward_body(base_ref, part_ref, recv_ref, rows_ref, out_ref, cast_ref, normed_ref, inv_ref):
    residual = base_ref[...] + part_ref[...] + recv_ref[...].astype(f32) + rows_ref[0:1, :]
    result, normed, inv_std = norm_forward(residual, rows_ref[1:2, :], rows_ref[2:3, :])
    out_ref[...] = result
    cast_ref[...] = result.astype(bf16)
    normed_ref[...] = normed
    inv_ref[...] = jnp.broadcast_to(inv_std, inv_ref.shape)


def norm_backward_math(incoming, normed_ref, inv_ref, rows_ref, out_ref, cast_ref, sum_ref):
    result, gain, shift = norm_backward(
        incoming, normed_ref[...], inv_ref[:, 0:1], rows_ref[1:2, :]
    )
    out_ref[...] = result
    cast_ref[...] = result.astype(bf16)
    sum_ref[0:1, :] = jnp.sum(result, axis=0, keepdims=True)
    sum_ref[1:2, :] = gain[None]
    sum_ref[2:3, :] = shift[None]


def norm_backward_body(incoming_ref, *refs):
    norm_backward_math(incoming_ref[...], *refs)


def norm_backward_add_body(base_ref, part_ref, recv_ref, *refs):
    incoming = base_ref[...] + part_ref[...] + recv_ref[...].astype(f32)
    norm_backward_math(incoming, *refs)


def product(left, right):
    return jnp.dot(left, right, preferred_element_type=f32)


def times_transpose(left, right):
    return contract(left, right, (1, 1))


def swap_dp(value, mask):
    size = lax.axis_size("dp")
    return lax.ppermute(value, "dp", [(at, at ^ mask) for at in range(size)])


def swap_tensor(value, mask):
    size = lax.axis_size("tensor")
    return lax.ppermute(value, "tensor", [(at, at ^ mask) for at in range(size)])


def gather_far(block):
    size = lax.axis_size("dp")
    return [block] + [swap_dp(block, mask) for mask in range(2, size, 2)]


def gather_group(far, parts):
    half = len(far) // 2
    rows = far[0].shape[0] // parts
    one, two = (
        jnp.concatenate(
            [
                entry[part * rows : (part + 1) * rows]
                for part in range(parts)
                for entry in far[at : at + half]
            ]
        )
        for at in (0, half)
    )
    one_x = swap_dp(one, 1)
    two_y = swap_tensor(two, 2)
    one_y = swap_tensor(one, 2)
    two_x = swap_dp(two, 1)
    one_xy = swap_tensor(one_x, 2)
    two_xy = swap_dp(two_y, 1)
    return (one, two, one_x, two_x, one_y, two_y, one_xy, two_xy)


def add_pair(left, right):
    return (left.astype(f32) + right.astype(f32)).astype(bf16)


def reduce_group(pieces, parts):
    one, two, one_x, two_x, one_y, two_y, one_xy, two_xy = pieces
    one_x = add_pair(one_x, swap_tensor(one_xy, 2))
    two_y = add_pair(two_y, swap_dp(two_xy, 1))
    one = add_pair(one, swap_tensor(one_y, 2))
    two = add_pair(two, swap_dp(two_x, 1))
    one = add_pair(one, swap_dp(one_x, 1))
    two = add_pair(two, swap_tensor(two_y, 2))
    half = lax.axis_size("dp") // 4
    span = one.shape[0] // parts
    rows = span // half
    total = None
    for at in range(2 * half):
        source = one if at < half else two
        start = (at % half) * rows
        chunk = [source[part * span + start : part * span + start + rows] for part in range(parts)]
        chunk = chunk[0] if parts == 1 else jnp.concatenate(chunk)
        if at == 0:
            total = chunk.astype(f32)
        else:
            total = total + swap_dp(chunk, 2 * at).astype(f32)
    return total


def mask_row():
    size = lax.axis_size("dp")
    half = size // 2
    at = lax.broadcasted_iota(jnp.int32, (1, size), 1)
    return lax.bitwise_xor(lax.axis_index("dp"), (at % half) * 2 + at // half)


def block_selector():
    size = lax.axis_size("dp")
    return lax.broadcasted_iota(jnp.int32, (size, size), 0) == mask_row()


def column_selector(width, block):
    half = lax.axis_size("dp") // 2
    column = lax.broadcasted_iota(jnp.int32, (1, width), 1)
    at = column // block
    actual = lax.bitwise_xor(lax.axis_index("dp"), (at % half) * 2 + at // half) * block + (
        column % block
    )
    return lax.broadcasted_iota(jnp.int32, (width, width), 0) == actual


def norm_step(base, part, recv, rows):
    count, model = base.shape
    outs = (
        shape(count, model, f32),
        shape(count, model, bf16),
        shape(count, model, f32),
        shape(count, 128, f32),
    )
    return run_kernel(norm_forward_body, outs, [], 0, base, part, recv, rows)


def forward_layer(hidden, hidden_cast, mix, rest, small):
    mix_bias, rise_bias, vectors = small
    count, model = hidden.shape
    full = 2 * count
    flops = 2 * full * model * model
    square = [pltpu.VMEM((model, model), bf16)]
    hidden_recv = swap_tensor(hidden_cast, 1)
    outs = (
        shape(full, model, bf16),
        shape(full, model, bf16),
        shape(full, 128, f32),
        shape(count, model, f32),
        shape(count, model, bf16),
    )
    side_a, side_b, log_total, part, send = run_kernel(
        attend_forward_body, outs, square, 4 * flops, hidden_cast, hidden_recv, mix_bias, *mix
    )
    first_norm, first_cast, normed_one, inv_one = norm_step(
        hidden, part, swap_tensor(send, 1), vectors[:3]
    )
    first_recv = swap_tensor(first_cast, 1)
    outs = (
        shape(full, model, f32),
        shape(full, model, f32),
        shape(full, model, bf16),
        shape(full, model, bf16),
        shape(count, model, f32),
        shape(count, model, bf16),
    )
    slope_a, slope_b, act_a, act_b, part, send = run_kernel(
        hidden_forward_body, outs, square, 5 * flops, first_cast, first_recv, rise_bias, *rest
    )
    result, result_cast, normed_two, inv_two = norm_step(
        first_norm, part, swap_tensor(send, 1), vectors[3:]
    )
    stored = (
        hidden_cast,
        hidden_recv,
        side_a,
        side_b,
        log_total,
        normed_one,
        inv_one,
        first_cast,
        first_recv,
        slope_a,
        slope_b,
        act_a,
        act_b,
        normed_two,
        inv_two,
    )
    return (result, result_cast, stored)


def backward_layer(incoming, stored, mix, rest, small):
    (
        hidden_cast,
        hidden_recv,
        side_a,
        side_b,
        log_total,
        normed_one,
        inv_one,
        first_cast,
        first_recv,
        slope_a,
        slope_b,
        act_a,
        act_b,
        normed_two,
        inv_two,
    ) = stored
    vectors = small[2]
    count, model = normed_one.shape
    full = 2 * count
    flops = 2 * full * model * model
    square = [pltpu.VMEM((model, model), bf16)]
    norm_outs = (shape(count, model, f32), shape(count, model, bf16), shape(3, model, f32))
    body = norm_backward_body if len(incoming) == 1 else norm_backward_add_body
    second_grad, second_cast, sums_two = run_kernel(
        body, norm_outs, [], 0, *incoming, normed_two, inv_two, vectors[3:]
    )
    second_recv = swap_tensor(second_cast, 1)
    outs = (
        shape(full, model, bf16),
        shape(full, model, bf16),
        shape(2, model, f32),
        shape(count, model, f32),
        shape(count, model, bf16),
    )
    grad_a, grad_b, rise_sums, part, send = run_kernel(
        hidden_backward_body,
        outs,
        square,
        4 * flops,
        second_cast,
        second_recv,
        slope_a,
        slope_b,
        *rest,
    )
    recv = swap_tensor(send, 1)
    pieces = run_kernel(
        hidden_grad_body,
        [shape(model // 2, model, bf16)] * 8,
        [],
        4 * flops,
        first_cast,
        first_recv,
        second_cast,
        second_recv,
        grad_a,
        grad_b,
        act_a,
        act_b,
    )
    rest_grad = reduce_group(pieces, 2)
    first_grad, first_grad_cast, sums_one = run_kernel(
        norm_backward_add_body,
        norm_outs,
        [],
        0,
        second_grad,
        part,
        recv,
        normed_one,
        inv_one,
        vectors[:3],
    )
    first_grad_recv = swap_tensor(first_grad_cast, 1)
    grad_a, grad_b, mix_sums, part, send = run_kernel(
        attend_backward_body,
        outs,
        square,
        6 * flops,
        first_grad_cast,
        first_grad_recv,
        side_a,
        side_b,
        log_total,
        *mix,
    )
    recv = swap_tensor(send, 1)
    pieces = run_kernel(
        mix_grad_body,
        [shape(model // 4, model, bf16)] * 8,
        [],
        3 * flops,
        hidden_cast,
        hidden_recv,
        first_grad_cast,
        first_grad_recv,
        grad_a,
        grad_b,
        side_a,
        side_b,
    )
    mix_grad = reduce_group(pieces, 1)
    head = model // 4
    bias_grad = [
        (mix_sums[side, :head], mix_sums[side, 2 * head : 3 * head], rise_sums[side])
        for side in range(2)
    ]
    vector_grad = jnp.concatenate([sums_one, sums_two])
    return ((first_grad, part, recv), (mix_grad, rest_grad), vector_grad, bias_grad)


def adam_update(parameter, gradient, moments, learn_rate, decay_rate):
    first_mom = beta_one * moments[0] + (1.0 - beta_one) * gradient
    second_mom = beta_two * moments[1] + (1.0 - beta_two) * gradient * gradient
    direction = (
        first_mom
        / (1.0 - beta_one**ADAM_STEP)
        / (jnp.sqrt(second_mom / (1.0 - beta_two**ADAM_STEP)) + adam_eps)
    )
    return (
        parameter - learn_rate * (direction + decay_rate * parameter),
        jnp.stack([first_mom, second_mom]),
    )


def pack_mix(qkv, proj):
    parts = [qkv[at] for at in range(qkv.shape[0])] + [proj.T]
    return jnp.concatenate(parts, axis=1).astype(bf16)


def gather_small(qv_bias, up_bias, norm_vectors):
    layers, _, block = norm_vectors.shape
    size = lax.axis_size("dp")
    width = qv_bias.shape[2]
    packed = jnp.concatenate(
        [norm_vectors.reshape(1, -1), up_bias.reshape(1, -1), qv_bias.reshape(1, -1)], axis=1
    ).astype(bf16)
    near = jnp.concatenate(gather_far(packed))
    own = jnp.concatenate([near, swap_dp(near, 1)])
    rank = norm_vectors.size
    other = swap_tensor(own[:, rank:], 2)
    vectors = (
        own[:, :rank].reshape(size, layers, 6, block).transpose(1, 2, 0, 3).reshape(layers, 6, -1)
    ).astype(f32)
    selector = block_selector().astype(bf16)
    ups, queries, values = [], [], []
    for entry in (own[:, rank:], other):
        entry = product(selector, entry)
        up = entry[:, : up_bias.size].reshape(size, layers, block)
        ups.append(up.transpose(1, 0, 2).reshape(layers, -1))
        qv = entry[:, up_bias.size :].reshape(size, layers, 2, width)
        qv = qv.transpose(1, 2, 0, 3).reshape(layers, 2, -1)
        queries.append(qv[:, 0])
        values.append(qv[:, 1])
    blank = jnp.zeros_like(queries[0])
    mix = jnp.stack(
        [
            jnp.concatenate([query, blank, value, blank], axis=1)
            for query, value in zip(queries, values)
        ]
    )
    rise = jnp.stack(ups)
    return [(mix[:, at], rise[:, at], vectors[at]) for at in range(layers)]


def reduce_small(vector_grads, bias_grads, block, width):
    size = lax.axis_size("dp")
    layers = len(vector_grads)
    vectors = jnp.stack(vector_grads)
    vectors = vectors.reshape(layers * 6, size, block).transpose(1, 0, 2).reshape(size, -1)
    sides = []
    for side in range(2):
        parts = []
        for at in range(layers):
            query_sum, value_sum, up_sum = bias_grads[at][side]
            parts += [
                query_sum.reshape(size, width),
                value_sum.reshape(size, width),
                up_sum.reshape(size, block),
            ]
        sides.append(jnp.concatenate(parts, axis=1))
    selector = block_selector().astype(f32)
    placed = lax.dot_general(
        selector,
        jnp.concatenate(sides, axis=1),
        (((0,), (0,)), ((), ())),
        precision=lax.Precision.HIGHEST,
        preferred_element_type=f32,
    )
    span = sides[0].shape[1]
    vectors = vectors + swap_tensor(vectors, 1)
    received = swap_tensor(jnp.concatenate([vectors, placed[:, span:]], axis=1), 2)
    total = jnp.concatenate([vectors, placed[:, :span]], axis=1) + received
    half = size // 2
    total = total[:half] + swap_dp(total[half:], 1)
    result = total[0:1]
    for at in range(1, half):
        result = result + swap_dp(total[at : at + 1], 2 * at)
    result = result[0]
    rank = layers * 6 * block
    vector_grad = result[:rank].reshape(layers, 6, block)
    rest = result[rank:].reshape(layers, -1)
    qv_grad = rest[:, : 2 * width].reshape(layers, 2, width)
    return vector_grad, qv_grad, rest[:, 2 * width :]


def on_device(
    layer_input,
    out_grad,
    qkv_weight,
    qv_bias,
    proj_weight,
    up_weight,
    up_bias,
    down_weight,
    norm_vectors,
    qkv_moments,
    qvbias_moments,
    proj_moments,
    up_moments,
    upbias_moments,
    down_moments,
    vector_moments,
):
    layers = qkv_weight.shape[0]
    block = norm_vectors.shape[2]
    width = qv_bias.shape[2]
    mixed, rested = [], []
    gate = None
    for at in range(layers):
        mix_block = pack_mix(qkv_weight[at], proj_weight[at])
        rest_block = jnp.concatenate([up_weight[at], down_weight[at].T]).astype(bf16)
        if gate is not None:
            mix_block, rest_block, gate = lax.optimization_barrier((mix_block, rest_block, gate))
        far_mix = gather_far(mix_block)
        far_rest = gather_far(rest_block)
        gate = far_rest[1]
        mixed.append(gather_group(far_mix, 1))
        rested.append(gather_group(far_rest, 2))
    small = gather_small(qv_bias, up_bias, norm_vectors)
    rows, model = layer_input.shape
    selector = column_selector(model, block).astype(bf16)
    ordered = product(jnp.concatenate([layer_input, out_grad]), selector)
    hidden, incoming = ordered[:rows], (ordered[rows:],)
    hidden_cast = hidden.astype(bf16)
    stored_all = []
    for at in range(layers):
        hidden, hidden_cast, stored = forward_layer(
            hidden, hidden_cast, mixed[at], rested[at], small[at]
        )
        stored_all.append(stored)
    block_output = times_transpose(hidden_cast, selector).astype(bf16)
    reduced = [None] * layers
    vector_grads = [None] * layers
    bias_grads = [None] * layers
    for at in reversed(range(layers)):
        incoming, reduced[at], vector_grads[at], bias_grads[at] = backward_layer(
            incoming, stored_all[at], mixed[at], rested[at], small[at]
        )
    input_grad = lax.dot_general(
        incoming[0] + incoming[1] + incoming[2].astype(f32),
        selector.astype(f32),
        (((1,), (1,)), ((), ())),
        precision=lax.Precision.HIGHEST,
        preferred_element_type=f32,
    )
    vector_grad, qv_grad, up_bias_grad = reduce_small(vector_grads, bias_grads, block, width)
    head = qkv_weight.shape[3]
    qkv_grad = jnp.stack(
        [
            jnp.stack([entry[0][:, at * head : (at + 1) * head] for at in range(3)])
            for entry in reduced
        ]
    )
    proj_grad = jnp.stack([entry[0][:, 3 * head :].T for entry in reduced])
    up_grad = jnp.stack([entry[1][:block] for entry in reduced])
    down_grad = jnp.stack([entry[1][block:].T for entry in reduced])
    gradients = (qkv_grad, qv_grad, proj_grad, up_grad, up_bias_grad, down_grad, vector_grad)
    parameters = (qkv_weight, qv_bias, proj_weight, up_weight, up_bias, down_weight, norm_vectors)
    moment_list = (
        qkv_moments,
        qvbias_moments,
        proj_moments,
        up_moments,
        upbias_moments,
        down_moments,
        vector_moments,
    )
    rates = (
        rate_matrix,
        rate_vector,
        rate_output,
        rate_matrix,
        rate_vector,
        rate_matrix,
        rate_vector,
    )
    decays = (decay_matrix, 0.0, decay_matrix, decay_matrix, 0.0, decay_matrix, 0.0)
    results = [
        adam_update(
            parameters[member],
            gradients[member],
            moment_list[member],
            rates[member],
            decays[member],
        )
        for member in range(7)
    ]
    return (
        block_output,
        input_grad,
        *gradients,
        *(entry[0] for entry in results),
        *(entry[1] for entry in results),
    )


def solution(mesh):
    return jax.shard_map(
        on_device,
        mesh=mesh,
        in_specs=(
            P(("dp", "tensor"), None),
            P(("dp", "tensor"), None),
            P(None, None, "dp", "tensor"),
            P(None, None, ("tensor", "dp")),
            P(None, "tensor", "dp"),
            P(None, "dp", "tensor"),
            P(None, ("tensor", "dp")),
            P(None, "tensor", "dp"),
            P(None, None, "dp"),
            P(None, None, None, "dp", "tensor"),
            P(None, None, None, ("tensor", "dp")),
            P(None, None, "tensor", "dp"),
            P(None, None, "dp", "tensor"),
            P(None, None, ("tensor", "dp")),
            P(None, None, "tensor", "dp"),
            P(None, None, None, "dp"),
        ),
        out_specs=(
            P(("dp", "tensor"), None),
            P(("dp", "tensor"), None),
            P(None, None, "dp", "tensor"),
            P(None, None, ("tensor", "dp")),
            P(None, "tensor", "dp"),
            P(None, "dp", "tensor"),
            P(None, ("tensor", "dp")),
            P(None, "tensor", "dp"),
            P(None, None, "dp"),
            P(None, None, "dp", "tensor"),
            P(None, None, ("tensor", "dp")),
            P(None, "tensor", "dp"),
            P(None, "dp", "tensor"),
            P(None, ("tensor", "dp")),
            P(None, "tensor", "dp"),
            P(None, None, "dp"),
            P(None, None, None, "dp", "tensor"),
            P(None, None, None, ("tensor", "dp")),
            P(None, None, "tensor", "dp"),
            P(None, None, "dp", "tensor"),
            P(None, None, ("tensor", "dp")),
            P(None, None, "tensor", "dp"),
            P(None, None, None, "dp"),
        ),
        check_vma=False,
    )
```
